32 devices in a mesh: group: 4 (over x, core), seq: 8 (over z, y).
Axes of the slice: x: 2, y: 2, z: 4, core: 2. Of those that a mesh axis runs over, the one named last changes fastest.
Arguments:
- features: bfloat16 [16, 64, 16, 384], P('group', 'seq'), parts along dimension 0, may hold values from -6 to 6
- cotangent: bfloat16 [16, 64, 16, 192], P('group', 'seq'), parts along dimension 0, may hold values from -6 to 6
- conv_weight: bfloat16 [3, 3, 3, 384, 192], replicated, may hold values from -0.0625 to 0.0625
- patch_map: bfloat16 [1536, 4096], P('seq'), may hold values from -0.15625 to 0.15625
- qkv: bfloat16 [3, 4096, 4096], P(None, ('group', 'seq')), parts along dimension 1, may hold values from -122 to 122
Outputs:
- weight_grad: float32 [12, 3, 3, 384, 192], P('group'), parts along dimension 0
- grad_qkv: bfloat16 [3, 4096, 4096], P(None, ('group', 'seq')), parts along dimension 1
The draws below stay inside these ranges and needn't reach their ends.
There are 4 independent parts, one for each index of `group`. The reference program is written for one: setup_inputs(seed, part) draws one part's arguments, and reference() takes and returns one part's arrays. A program takes and returns all parts, laid end to end along the dimension named above; an argument that names none is the same for every part. Nothing has to cross between parts.
All inputs are finite; a program needn't handle non-finite values.
Results may differ from the reference program's by a relative error of at most 0.0075.
Values may be sent and summed in bfloat16 or wider, within the bound.
A program may use at most 128 MiB of HBM per device.

```python
import math
import jax
import jax.numpy as jnp
from jax import lax

CIN = 384
COUT = 192
HEADS = 32
FRAMES = 4
COLS = 16
HEIGHT = 64
PATCH = 1536
INNER = 4096
SEQUENCE = 1024


def draw_qkv(key, part):
    base = jnp.clip(jax.random.normal(key, (3, SEQUENCE, INNER), jnp.float32), -4.5, 4.5)
    return base.astype(jnp.bfloat16)


def block_levels(own_key, dims, split, least, high):
    factor_of, own = 1.0, jax.random.fold_in(own_key, 6)
    for axis_at, shards_of in split:
        steps = jnp.exp(jax.random.uniform(jax.random.fold_in(own, axis_at), (shards_of,), jnp.float32, least / len(split), high / len(split)))
        factor_of = factor_of * jnp.repeat(steps, dims[axis_at] // shards_of).reshape([-1 if axis == axis_at else 1 for axis in range(len(dims))])
    return factor_of


def gaussian(rng, shape, scale, reach, pieces=(), held_as=jnp.bfloat16):
    gain = block_levels(rng, shape, pieces, -0.22, 0.18) if pieces else 1.0
    values = jax.random.normal(rng, shape, jnp.float32) * scale * gain
    return jnp.minimum(jnp.maximum(values, -reach), reach).astype(held_as)


def setup_inputs(seed: int = 0, part: int = 0) -> dict:
    key_list = jax.random.split(jax.random.key(seed), 6)
    own_keys = jax.random.split(jax.random.fold_in(key_list[5], part), 6)
    return {
        "features": gaussian(own_keys[0], (FRAMES, HEIGHT, COLS, CIN), 1.0, 6.0, ((1, 8),)),
        "cotangent": gaussian(own_keys[1], (FRAMES, HEIGHT, COLS, COUT), 1.0, 6.0, ((1, 8),)),
        "conv_weight": gaussian(key_list[2], (3, 3, 3, CIN, COUT), (27 * CIN) ** -0.5, 0.0625),
        "patch_map": gaussian(key_list[3], (PATCH, INNER), PATCH ** -0.5, 0.15625, ((0, 8),)),
        "qkv": draw_qkv(jax.random.fold_in(jax.random.fold_in(key_list[5], part), 71), part),
    }


def attend_head(query, keys, values, grad_out):
    width = query.shape[1]
    scale = 1.0 / math.sqrt(width)
    scores = lax.dot_general(query, keys, (((1,), (1,)), ((), ())), preferred_element_type=jnp.float32) * scale
    top = lax.optimization_barrier(jnp.max(scores, axis=1, keepdims=True))
    expo = jnp.exp(scores - top)
    probs = expo / lax.optimization_barrier(jnp.sum(expo, axis=1, keepdims=True))
    dprob = lax.dot_general(grad_out, values, (((1,), (1,)), ((), ())), preferred_element_type=jnp.float32)
    delta = lax.optimization_barrier(jnp.sum(probs * dprob, axis=1, keepdims=True))
    dscore = (probs * (dprob - delta) * scale).astype(jnp.bfloat16)
    pround = probs.astype(jnp.bfloat16)
    dquery = jnp.dot(dscore, keys, preferred_element_type=jnp.float32).astype(jnp.bfloat16)
    dkeys = lax.dot_general(dscore, query, (((0,), (0,)), ((), ())), preferred_element_type=jnp.float32).astype(jnp.bfloat16)
    dvalues = lax.dot_general(pround, grad_out, (((0,), (0,)), ((), ())), preferred_element_type=jnp.float32).astype(jnp.bfloat16)
    return (dquery, dkeys, dvalues)

def reference(features, cotangent, conv_weight, patch_map, qkv):
    frames, height, cols, cin = features.shape
    cout = cotangent.shape[3]
    padded = jnp.pad(cotangent, ((0, 2), (1, 1), (1, 1), (0, 0)))
    flat_in = features.reshape(-1, cin)
    grad_in = jnp.zeros((frames * height * cols, cin), jnp.float32)
    taps = []
    for tap_t in range(3):
        for tap_h in range(3):
            for tap_w in range(3):
                shifted = padded[2 - tap_t:2 - tap_t + frames, 2 - tap_h:2 - tap_h + height, 2 - tap_w:2 - tap_w + cols]
                shifted = shifted.reshape(-1, cout)
                grad_in = grad_in + lax.dot_general(shifted, conv_weight[tap_t, tap_h, tap_w], (((1,), (1,)), ((), ())), preferred_element_type=jnp.float32)
                taps.append(lax.dot_general(flat_in, shifted, (((0,), (0,)), ((), ())), preferred_element_type=jnp.float32))
    weight_grad = jnp.stack(taps).reshape(3, 3, 3, cin, cout) * (1.0 / math.sqrt(frames * height * cols))
    grad_in = grad_in.reshape(frames, height // 2, 2, cols // 2, 2, cin).transpose(1, 0, 3, 2, 4, 5)
    patches = grad_in.reshape(-1, 4 * cin).astype(jnp.bfloat16)
    grad_out = jnp.dot(patches, patch_map, preferred_element_type=jnp.float32).astype(jnp.bfloat16)
    length = qkv.shape[1]
    heads_n = HEADS
    head_dim = qkv.shape[2] // heads_n
    stacked = qkv.reshape(3, length, heads_n, head_dim).transpose(0, 2, 1, 3)
    grads = grad_out.reshape(length, heads_n, head_dim).transpose(1, 0, 2)

    def one_head(packed):
        return attend_head(packed[0], packed[1], packed[2], packed[3])
    dquery, dkeys, dvalues = lax.map(one_head, (stacked[0], stacked[1], stacked[2], grads))
    result = jnp.stack([dquery, dkeys, dvalues]).transpose(0, 2, 1, 3).reshape(3, length, heads_n * head_dim)
    return (weight_grad, result)
```

```python
import math

import jax
import jax.numpy as jnp
from jax import lax
from jax.experimental import pallas as pl
from jax.experimental.pallas import tpu as pltpu
from jax.sharding import PartitionSpec as P

HEADS = 32
TILE = 32
LIMIT = 60 * 1024 * 1024


def flops(count, moved):
    return pl.CostEstimate(flops=count, bytes_accessed=moved, transcendentals=0)


def grad_out_kernel(x_ref, w_ref, map_ref, out_ref, acc_ref):
    frames, span, wide = x_ref.shape[1], x_ref.shape[2], x_ref.shape[3]
    double = w_ref.shape[2]
    tap_h = pl.program_id(1)

    for side in range(2):
        for tap_t in (2, 1, 0):
            live = frames - 2 + tap_t
            rows = x_ref[side + 2 - tap_h, 2 - tap_t :].reshape(live * span, wide)
            part = lax.dot_general(
                rows, w_ref[tap_t, 0], (((1,), (1,)), ((), ())), preferred_element_type=jnp.float32
            )
            if tap_t == 2:

                @pl.when(tap_h == 0)
                def _():
                    acc_ref[side] = part

                @pl.when(tap_h > 0)
                def _():
                    acc_ref[side] += part

            else:
                acc_ref[side, : live * span] += part

    @pl.when(tap_h == 2)
    def _():
        wide_out = out_ref.shape[1]
        total = jnp.dot(
            acc_ref[0].astype(jnp.bfloat16), map_ref[:double], preferred_element_type=jnp.float32
        ) + jnp.dot(
            acc_ref[1].astype(jnp.bfloat16), map_ref[double:], preferred_element_type=jnp.float32
        )
        each = span // TILE
        total = total.reshape(frames, TILE, each, wide_out).transpose(1, 0, 2, 3)
        out_ref[...] = total.reshape(frames * span, wide_out).astype(jnp.bfloat16)


def weight_kernel(scale, blocks, feat_ref, x_ref, out_ref, turned_ref):
    frames, span, wide = x_ref.shape[1], x_ref.shape[2], x_ref.shape[3]
    double = feat_ref.shape[4]
    cin, cout = double // 2, wide // 4
    tap_h = pl.program_id(0)
    block = pl.program_id(1)

    def turn():
        for side in range(2):
            for frame in range(frames):
                turned_ref[side, :, frame * span : (frame + 1) * span] = (
                    feat_ref[:, side, frame].reshape(span, double).T
                )

    if blocks == 1:
        pl.when(tap_h == 0)(turn)
    else:
        turn()
    for tap_t in range(3):
        live = frames - 2 + tap_t
        prod = None
        for side in range(2):
            rows = x_ref[side + 2 - tap_h, 2 - tap_t :].reshape(live * span, wide)
            part = jnp.dot(
                turned_ref[side, :, : live * span], rows, preferred_element_type=jnp.float32
            )
            prod = part if prod is None else prod + part
        for tap_w in range(3):
            even = prod[:cin, cout * (2 - tap_w) : cout * (3 - tap_w)]
            odd = prod[cin:, cout * (3 - tap_w) : cout * (4 - tap_w)]
            value = (even + odd) * scale
            if blocks == 1:
                out_ref[tap_t, 0, tap_w] = value
            else:

                @pl.when(block == 0)
                def _():
                    out_ref[tap_t, 0, tap_w] = value

                @pl.when(block > 0)
                def _():
                    out_ref[tap_t, 0, tap_w] += value


def attention_kernel(step, qkv_ref, grad_ref, out_ref, dk_ref, dv_ref):
    shards, _, rows, width = qkv_ref.shape
    length = shards * rows
    scale = 1.0 / math.sqrt(width)
    keys = qkv_ref[:, 1].reshape(length, width)
    values = qkv_ref[:, 2].reshape(length, width)
    keys_t = keys.T
    span = step * rows

    def block(index, first):
        query = qkv_ref[pl.ds(index * step, step), 0].reshape(span, width)
        grads = grad_ref[pl.ds(pl.multiple_of(index * span, span), span), :]
        scores = lax.dot_general(
            keys, query, (((1,), (1,)), ((), ())), preferred_element_type=jnp.float32
        )
        top = jnp.max(scores, axis=0, keepdims=True)
        expo = jnp.exp((scores - top) * scale)
        probs = expo * (1.0 / jnp.sum(expo, axis=0, keepdims=True))
        dprob = lax.dot_general(
            values, grads, (((1,), (1,)), ((), ())), preferred_element_type=jnp.float32
        )
        delta = jnp.sum(probs * dprob, axis=0, keepdims=True)
        dscore = (probs * (dprob - delta)).astype(jnp.bfloat16)
        dquery = jnp.dot(keys_t, dscore, preferred_element_type=jnp.float32) * scale
        out_ref[pl.ds(index * step, step), 0] = (
            dquery.T.reshape(step, rows, width).astype(jnp.bfloat16)
        )
        part_k = jnp.dot(dscore, query, preferred_element_type=jnp.float32)
        part_v = jnp.dot(probs.astype(jnp.bfloat16), grads, preferred_element_type=jnp.float32)
        if first:
            dk_ref[...] = part_k
            dv_ref[...] = part_v
        else:
            dk_ref[...] += part_k
            dv_ref[...] += part_v

    count = shards // step
    if count <= 4:
        for index in range(count):
            block(index, index == 0)
    else:
        block(0, True)

        @pl.loop(1, count)
        def _(index):
            block(index, False)

    out_ref[:, 1] = (dk_ref[...] * scale).reshape(shards, rows, width).astype(jnp.bfloat16)
    out_ref[:, 2] = dv_ref[...].reshape(shards, rows, width).astype(jnp.bfloat16)


def per_device(features, cotangent, conv_weight, patch_map, qkv):
    frames, rows_here, cols, cin = features.shape
    cout = cotangent.shape[3]
    count = lax.axis_size("seq")
    parts = lax.axis_size("group")
    half, pairs = cols // 2, rows_here // 2
    pairs_all = pairs * count
    tokens_here, inner = qkv.shape[1], qkv.shape[2]
    length = tokens_here * count
    mine = inner // count
    head_dim = inner // HEADS

    cot = cotangent.reshape(frames, pairs, 2, half, 2 * cout).transpose(2, 0, 1, 3, 4)
    cot = lax.all_gather(cot.reshape(-1, 2 * cout), "seq", axis=0, tiled=True)
    sent = qkv.reshape(3, tokens_here, count, mine).transpose(2, 0, 1, 3)
    moved = lax.all_to_all(sent, "seq", split_axis=0, concat_axis=0, tiled=True)
    share = mine // parts
    depth = patch_map.shape[0]
    member = lax.axis_index("group")
    piece = lax.dynamic_index_in_dim(
        patch_map.reshape(depth, count, parts, share), member, axis=2, keepdims=False
    )
    piece = lax.all_to_all(
        piece.transpose(1, 0, 2), "seq", split_axis=0, concat_axis=0, tiled=True
    ).reshape(count * depth, share)
    columns = lax.all_gather(piece, "group", axis=0, tiled=False)
    columns = columns.transpose(1, 0, 2).reshape(count * depth, mine)
    feat = features.reshape(frames, pairs, 2, half, 2 * cin).transpose(2, 0, 1, 3, 4)
    feat = lax.all_gather(feat.reshape(-1, 2 * cin), "seq", axis=0, tiled=True)
    feat = feat.reshape(count, 2, frames, pairs * half, 2 * cin)

    full = cot.reshape(count, 2, frames, pairs, half, 2 * cout).transpose(1, 2, 0, 3, 4, 5)
    full = full.reshape(2, frames, pairs_all, half, 2 * cout)
    left = jnp.pad(full[:, :, :, :-1, cout:], ((0, 0), (0, 0), (0, 0), (1, 0), (0, 0)))
    right = jnp.pad(full[:, :, :, 1:, :cout], ((0, 0), (0, 0), (0, 0), (0, 1), (0, 0)))
    wide = jnp.concatenate([left, full, right], axis=-1)
    above = jnp.pad(wide[1][:, :-1], ((0, 0), (1, 0), (0, 0), (0, 0)))
    below = jnp.pad(wide[0][:, 1:], ((0, 0), (0, 1), (0, 0), (0, 0)))
    shifts = jnp.stack([above, wide[0], wide[1], below])
    shifts = shifts.reshape(4, frames, pairs_all * half, 4 * cout)

    taps = [conv_weight[:, :, tap_w] for tap_w in range(3)]
    blank = jnp.zeros_like(taps[0])
    big = jnp.concatenate(
        [
            jnp.concatenate([taps[2], taps[1], taps[0], blank], axis=-1),
            jnp.concatenate([blank, taps[2], taps[1], taps[0]], axis=-1),
        ],
        axis=2,
    )

    blocks = pairs_all // TILE
    span = TILE * half
    work = 2 * 9 * 3 * 2 * pairs_all * half * (2 * cin) * (4 * cout)
    x_block = pl.BlockSpec((4, frames, span, 4 * cout), lambda blk, tap: (0, 0, blk, 0))
    grad_out = pl.pallas_call(
        grad_out_kernel,
        grid=(blocks, 3),
        in_specs=[
            x_block,
            pl.BlockSpec((3, 1, 2 * cin, 4 * cout), lambda blk, tap: (0, tap, 0, 0)),
            pl.BlockSpec((count * depth, mine), lambda blk, tap: (0, 0)),
        ],
        out_specs=pl.BlockSpec((frames * span, mine), lambda blk, tap: (blk, 0)),
        out_shape=jax.ShapeDtypeStruct((length, mine), jnp.bfloat16),
        scratch_shapes=[pltpu.VMEM((2, frames * span, 2 * cin), jnp.float32)],
        compiler_params=pltpu.CompilerParams(vmem_limit_bytes=LIMIT),
        cost_estimate=flops(work, 20 << 20),
        name="grad_out",
    )(shifts, big, columns)

    step = max(1, 256 // tokens_here)
    head_block = pl.BlockSpec((count, 3, tokens_here, head_dim), lambda head: (0, 0, 0, head))
    heads_here = HEADS // count
    result = pl.pallas_call(
        lambda *refs: attention_kernel(step, *refs),
        grid=(heads_here,),
        in_specs=[head_block, pl.BlockSpec((length, head_dim), lambda head: (0, head))],
        out_specs=head_block,
        out_shape=jax.ShapeDtypeStruct((count, 3, tokens_here, mine), jnp.bfloat16),
        scratch_shapes=[pltpu.VMEM((length, head_dim), jnp.float32)] * 2,
        compiler_params=pltpu.CompilerParams(vmem_limit_bytes=LIMIT),
        cost_estimate=flops(heads_here * 20 * length * length * head_dim, 8 << 20),
        name="attention",
    )(moved, grad_out)

    shifts, result = lax.optimization_barrier((shifts, result))
    back = lax.all_to_all(result, "seq", split_axis=0, concat_axis=0, tiled=True)

    scale = 1.0 / math.sqrt(frames * rows_here * count * cols)
    shards = TILE // pairs
    weight_grad = pl.pallas_call(
        lambda *refs: weight_kernel(scale, blocks, *refs),
        grid=(3, blocks),
        in_specs=[
            pl.BlockSpec(
                (shards, 2, frames, pairs * half, 2 * cin), lambda tap, blk: (blk, 0, 0, 0, 0)
            ),
            pl.BlockSpec((4, frames, span, 4 * cout), lambda tap, blk: (0, 0, blk, 0)),
        ],
        out_specs=pl.BlockSpec((3, 1, 3, cin, cout), lambda tap, blk: (0, tap, 0, 0, 0)),
        out_shape=jax.ShapeDtypeStruct((3, 3, 3, cin, cout), jnp.float32),
        scratch_shapes=[pltpu.VMEM((2, 2 * cin, frames * span), jnp.bfloat16)],
        compiler_params=pltpu.CompilerParams(vmem_limit_bytes=LIMIT),
        cost_estimate=flops(work, 20 << 20),
        name="weight_grad",
    )(feat, shifts)
    back = back.transpose(1, 2, 0, 3).reshape(3, tokens_here, inner)
    return (weight_grad, back)


def solution(mesh):
    placed = (
        P("group", "seq", None, None),
        P("group", "seq", None, None),
        P(),
        P("seq", None),
        P(None, ("group", "seq"), None),
    )
    return jax.shard_map(
        per_device,
        mesh=mesh,
        in_specs=placed,
        out_specs=(P("group", None, None, None, None), P(None, ("group", "seq"), None)),
        check_vma=False,
    )
```

```python
import math

import jax
import jax.numpy as jnp
from jax import lax
from jax.experimental import pallas as pl
from jax.experimental.pallas import tpu as pltpu
from jax.sharding import PartitionSpec as P

HEADS = 32
TILE = 32
LIMIT = 60 * 1024 * 1024


def flops(count, moved):
    return pl.CostEstimate(flops=count, bytes_accessed=moved, transcendentals=0)


def patches_kernel(x_ref, w_ref, out_ref, acc_ref, mix_ref):
    frames, span, wide = x_ref.shape[1], x_ref.shape[2], x_ref.shape[3]
    cout, cin = w_ref.shape[3], w_ref.shape[4]
    tap_h = pl.program_id(1)

    for tap_t in range(3):
        for even in range(2):
            lanes = slice(even * cin, (even + 1) * cin)
            for place in range(4):
                tap_w = 2 + even - place
                rows = slice(place * cout, (place + 1) * cout)
                if 0 <= tap_w <= 2:
                    mix_ref[tap_t, rows, lanes] = w_ref[tap_t, 0, tap_w]
                else:
                    mix_ref[tap_t, rows, lanes] = jnp.zeros((cout, cin), mix_ref.dtype)
    for side in range(2):
        for tap_t in (2, 1, 0):
            live = frames - 2 + tap_t
            rows = x_ref[side + 2 - tap_h, 2 - tap_t :].reshape(live * span, wide)
            part = jnp.dot(rows, mix_ref[tap_t], preferred_element_type=jnp.float32)
            if tap_t == 2:

                @pl.when(tap_h == 0)
                def _():
                    acc_ref[side] = part

                @pl.when(tap_h > 0)
                def _():
                    acc_ref[side] += part

            else:
                acc_ref[side, : live * span] += part

    @pl.when(tap_h == 2)
    def _():
        each = span // TILE
        for side in range(2):
            total = acc_ref[side].reshape(frames, TILE, each, 2 * cin).transpose(1, 0, 2, 3)
            out_ref[:, side * 2 * cin : (side + 1) * 2 * cin] = total.reshape(
                frames * span, 2 * cin
            ).astype(jnp.bfloat16)


def weight_kernel(scale, blocks, feat_ref, x_ref, out_ref, turned_ref, flat_ref):
    frames, span, wide = x_ref.shape[1], x_ref.shape[2], x_ref.shape[3]
    double = feat_ref.shape[4]
    cin, cout = double // 2, wide // 4
    tap_h = pl.program_id(0)
    block = pl.program_id(1)

    def turn():
        for frame in range(frames):
            part = slice(frame * span, (frame + 1) * span)
            for side in range(2):
                flat_ref[side, part] = feat_ref[:, side, frame].reshape(span, double)
            for shift in range(4):
                turned_ref[shift, :, part] = x_ref[shift, frame].T

    if blocks == 1:
        pl.when(tap_h == 0)(turn)
    else:
        turn()
    for tap_t in range(3):
        live = frames - 2 + tap_t
        prod = None
        for side in range(2):
            part = jnp.dot(
                turned_ref[side + 2 - tap_h, :, (2 - tap_t) * span :],
                flat_ref[side, : live * span],
                preferred_element_type=jnp.float32,
            )
            prod = part if prod is None else prod + part
        for tap_w in range(3):
            even = prod[cout * (2 - tap_w) : cout * (3 - tap_w), :cin]
            odd = prod[cout * (3 - tap_w) : cout * (4 - tap_w), cin:]
            value = (even + odd) * scale
            if blocks == 1:
                out_ref[tap_t, 0, tap_w] = value
            else:

                @pl.when(block == 0)
                def _():
                    out_ref[tap_t, 0, tap_w] = value

                @pl.when(block > 0)
                def _():
                    out_ref[tap_t, 0, tap_w] += value


def split_kernel(in_ref, out_ref):
    out_ref[0] = in_ref[...]


def join_kernel(in_ref, out_ref):
    out_ref[...] = in_ref[0]


def exchange(pieces, axis):
    count = lax.axis_size(axis)
    me = lax.axis_index(axis)
    got = [lax.dynamic_index_in_dim(pieces, me, 0, keepdims=False)]
    for away in range(1, count):
        chunk = lax.dynamic_index_in_dim(pieces, (me + away) % count, 0, keepdims=False)
        got.append(lax.ppermute(chunk, axis, [(i, (i + away) % count) for i in range(count)]))
    return arrange(got, me, count)


def gather(piece, axis):
    count = lax.axis_size(axis)
    me = lax.axis_index(axis)
    got = [piece]
    for away in range(1, count):
        got.append(lax.ppermute(piece, axis, [(i, (i + away) % count) for i in range(count)]))
    return arrange(got, me, count)


def arrange(got, me, count):
    result = jnp.zeros((count,) + got[0].shape, got[0].dtype)
    for away in range(count):
        result = lax.dynamic_update_index_in_dim(result, got[away], (me + count - away) % count, 0)
    return result


def attention_kernel(step, qkv_ref, grad_ref, out_ref, dk_ref, dv_ref):
    shards, _, rows, width = qkv_ref.shape
    length = shards * rows
    scale = 1.0 / math.sqrt(width)
    keys = qkv_ref[:, 1].reshape(length, width)
    values = qkv_ref[:, 2].reshape(length, width)
    keys_t = keys.T
    span = step * rows

    def block(index, first):
        query = qkv_ref[pl.ds(index * step, step), 0].reshape(span, width)
        grads = grad_ref[pl.ds(pl.multiple_of(index * span, span), span), :]
        scores = lax.dot_general(
            keys, query, (((1,), (1,)), ((), ())), preferred_element_type=jnp.float32
        )
        top = jnp.max(scores, axis=0, keepdims=True)
        expo = jnp.exp((scores - top) * scale)
        probs = expo * (1.0 / jnp.sum(expo, axis=0, keepdims=True))
        dprob = lax.dot_general(
            values, grads, (((1,), (1,)), ((), ())), preferred_element_type=jnp.float32
        )
        delta = jnp.sum(probs * dprob, axis=0, keepdims=True)
        dscore = (probs * (dprob - delta)).astype(jnp.bfloat16)
        dquery = jnp.dot(keys_t, dscore, preferred_element_type=jnp.float32) * scale
        out_ref[pl.ds(index * step, step), 0] = (
            dquery.T.reshape(step, rows, width).astype(jnp.bfloat16)
        )
        part_k = jnp.dot(dscore, query, preferred_element_type=jnp.float32)
        part_v = jnp.dot(probs.astype(jnp.bfloat16), grads, preferred_element_type=jnp.float32)
        if first:
            dk_ref[...] = part_k
            dv_ref[...] = part_v
        else:
            dk_ref[...] += part_k
            dv_ref[...] += part_v

    count = shards // step
    if count <= 4:
        for index in range(count):
            block(index, index == 0)
    else:
        block(0, True)

        @pl.loop(1, count)
        def _(index):
            block(index, False)

    out_ref[:, 1] = (dk_ref[...] * scale).reshape(shards, rows, width).astype(jnp.bfloat16)
    out_ref[:, 2] = dv_ref[...].reshape(shards, rows, width).astype(jnp.bfloat16)


def per_device(features, cotangent, conv_weight, patch_map, qkv):
    frames, rows_here, cols, cin = features.shape
    cout = cotangent.shape[3]
    count = lax.axis_size("seq")
    parts = lax.axis_size("group")
    half, pairs = cols // 2, rows_here // 2
    pairs_all = pairs * count
    tokens_here, inner = qkv.shape[1], qkv.shape[2]
    length = tokens_here * count
    mine = inner // count
    head_dim = inner // HEADS

    cot = cotangent.reshape(frames, pairs, 2, half, 2 * cout).transpose(2, 0, 1, 3, 4)
    cot = lax.all_gather(cot.reshape(-1, 2 * cout), "seq", axis=0, tiled=True)
    near = pl.BlockSpec((3, tokens_here, mine), lambda to: (0, 0, to))
    far = pl.BlockSpec((1, 3, tokens_here, mine), lambda to: (to, 0, 0, 0))
    sent = pl.pallas_call(
        split_kernel,
        grid=(count,),
        in_specs=[near],
        out_specs=far,
        out_shape=jax.ShapeDtypeStruct((count, 3, tokens_here, mine), qkv.dtype),
        cost_estimate=flops(0, 6 << 20),
        name="split",
    )(qkv)
    moved = lax.all_to_all(sent, "seq", split_axis=0, concat_axis=0, tiled=True)
    share = mine // parts
    depth = patch_map.shape[0]
    member = lax.axis_index("group")
    piece = lax.dynamic_index_in_dim(
        patch_map.reshape(depth, count, parts, share), member, axis=2, keepdims=False
    )
    piece = exchange(piece.transpose(1, 0, 2), "seq").reshape(count * depth, share)
    columns = gather(piece, "group")
    columns = columns.transpose(1, 0, 2).reshape(count * depth, mine)
    feat = features.reshape(frames, pairs, 2, half, 2 * cin).transpose(2, 0, 1, 3, 4)
    full = cot.reshape(count, 2, frames, pairs, half, 2 * cout).transpose(1, 2, 0, 3, 4, 5)
    full = full.reshape(2, frames, pairs_all, half, 2 * cout)
    left = jnp.pad(full[:, :, :, :-1, cout:], ((0, 0), (0, 0), (0, 0), (1, 0), (0, 0)))
    right = jnp.pad(full[:, :, :, 1:, :cout], ((0, 0), (0, 0), (0, 0), (0, 1), (0, 0)))
    wide = jnp.concatenate([left, full, right], axis=-1)
    above = jnp.pad(wide[1][:, :-1], ((0, 0), (1, 0), (0, 0), (0, 0)))
    below = jnp.pad(wide[0][:, 1:], ((0, 0), (0, 1), (0, 0), (0, 0)))
    shifts = jnp.stack([above, wide[0], wide[1], below])
    shifts = shifts.reshape(4, frames, pairs_all * half, 4 * cout)

    blocks = pairs_all // TILE
    span = TILE * half
    work = 2 * 9 * 3 * 2 * pairs_all * half * (2 * cin) * (4 * cout)
    x_block = pl.BlockSpec((4, frames, span, 4 * cout), lambda blk, tap: (0, 0, blk, 0))
    patches = pl.pallas_call(
        patches_kernel,
        grid=(blocks, 3),
        in_specs=[
            x_block,
            pl.BlockSpec((3, 1, 3, cout, cin), lambda blk, tap: (0, tap, 0, 0, 0)),
        ],
        out_specs=pl.BlockSpec((frames * span, 4 * cin), lambda blk, tap: (blk, 0)),
        out_shape=jax.ShapeDtypeStruct((length, 4 * cin), jnp.bfloat16),
        scratch_shapes=[
            pltpu.VMEM((2, frames * span, 2 * cin), jnp.float32),
            pltpu.VMEM((3, 4 * cout, 2 * cin), jnp.bfloat16),
        ],
        compiler_params=pltpu.CompilerParams(vmem_limit_bytes=LIMIT),
        cost_estimate=flops(work, 20 << 20),
        name="patches",
    )(shifts, conv_weight.transpose(0, 1, 2, 4, 3))
    feat, patches = lax.optimization_barrier((feat.reshape(-1, 2 * cin), patches))
    feat = lax.all_gather(feat, "seq", axis=0, tiled=True)
    feat = feat.reshape(count, 2, frames, pairs * half, 2 * cin)
    grad_out = jnp.dot(patches, columns, preferred_element_type=jnp.float32).astype(jnp.bfloat16)

    step = max(1, 256 // tokens_here)
    head_block = pl.BlockSpec((count, 3, tokens_here, head_dim), lambda head: (0, 0, 0, head))
    heads_here = HEADS // count
    result = pl.pallas_call(
        lambda *refs: attention_kernel(step, *refs),
        grid=(heads_here,),
        in_specs=[head_block, pl.BlockSpec((length, head_dim), lambda head: (0, head))],
        out_specs=head_block,
        out_shape=jax.ShapeDtypeStruct((count, 3, tokens_here, mine), jnp.bfloat16),
        scratch_shapes=[pltpu.VMEM((length, head_dim), jnp.float32)] * 2,
        compiler_params=pltpu.CompilerParams(vmem_limit_bytes=LIMIT),
        cost_estimate=flops(heads_here * 20 * length * length * head_dim, 8 << 20),
        name="attention",
    )(moved, grad_out)

    shifts, result = lax.optimization_barrier((shifts, result))
    back = lax.all_to_all(result, "seq", split_axis=0, concat_axis=0, tiled=True)

    scale = 1.0 / math.sqrt(frames * rows_here * count * cols)
    shards = TILE // pairs
    weight_grad = pl.pallas_call(
        lambda *refs: weight_kernel(scale, blocks, *refs),
        grid=(3, blocks),
        in_specs=[
            pl.BlockSpec(
                (shards, 2, frames, pairs * half, 2 * cin), lambda tap, blk: (blk, 0, 0, 0, 0)
            ),
            pl.BlockSpec((4, frames, span, 4 * cout), lambda tap, blk: (0, 0, blk, 0)),
        ],
        out_specs=pl.BlockSpec((3, 1, 3, cout, cin), lambda tap, blk: (0, tap, 0, 0, 0)),
        out_shape=jax.ShapeDtypeStruct((3, 3, 3, cout, cin), jnp.float32),
        scratch_shapes=[
            pltpu.VMEM((4, 4 * cout, frames * span), jnp.bfloat16),
            pltpu.VMEM((2, frames * span, 2 * cin), jnp.bfloat16),
        ],
        compiler_params=pltpu.CompilerParams(vmem_limit_bytes=LIMIT),
        cost_estimate=flops(work, 20 << 20),
        name="weight_grad",
    )(feat, shifts)
    back = pl.pallas_call(
        join_kernel,
        grid=(count,),
        in_specs=[far],
        out_specs=near,
        out_shape=jax.ShapeDtypeStruct((3, tokens_here, inner), back.dtype),
        cost_estimate=flops(0, 6 << 20),
        name="join",
    )(back)
    return (weight_grad.transpose(0, 1, 2, 4, 3), back)


def solution(mesh):
    placed = (
        P("group", "seq", None, None),
        P("group", "seq", None, None),
        P(),
        P("seq", None),
        P(None, ("group", "seq"), None),
    )
    return jax.shard_map(
        per_device,
        mesh=mesh,
        in_specs=placed,
        out_specs=(P("group", None, None, None, None), P(None, ("group", "seq"), None)),
        check_vma=False,
    )
```
